32 devices in a mesh: day: 2 (over x), row: 16 (over z, y, core).
Axes of the slice: x: 2, y: 2, z: 4, core: 2. Of those that a mesh axis runs over, the one named last changes fastest.
Arguments:
- spectra: bfloat16 [4096, 2, 2, 4096], P(('day', 'row')), parts along dimension 0, may hold values from -110 to 110
- pair_channels: int32 [64, 128, 2], P('row'), may hold values from 0 to 2047, as said below
- pair_live: int32 [64, 128], P('row'), may hold values from 0 to 1, as said below
Outputs:
- correlations: float32 [128, 128, 512], P(('day', 'row')), parts along dimension 0
The draws below stay inside these ranges and needn't reach their ends.
There are 2 independent parts, one for each index of `day`. The reference program is written for one: setup_inputs(seed, part) draws one part's arguments, and reference() takes and returns one part's arrays. A program takes and returns all parts, laid end to end along the dimension named above; an argument that names none is the same for every part. Nothing has to cross between parts.
Inputs may be any that keep to these rules, and one draw needn't show every extreme that they name: `pair_channels`: pair slots of device i of row are tiles i * 4 to (i + 1) * 4 - 1; their first channels are that device's own channels i * 128 to (i + 1) * 128 - 1, and their second channels lie within 128 channels of the first; distances of exactly 128 occur on both sides. `pair_live`: in each device's pair slots (tile by tile, pair by pair) the live slots come first and the padding after; every device has 128 live slots or more, and one device's slots are all live.
All inputs are finite; a program needn't handle non-finite values.
Results may differ from the reference program's by a relative error of at most 0.003.
Values may be sent and summed in bfloat16 or wider, within the bound.
A program may use at most 192 MiB of HBM per device.

```python
import math
import jax
import jax.numpy as jnp
from jax import lax

CH_DEV = 128
TILE_SLOTS = 4
WIN = 2
FREQ = 4096
BAND = 64
LAGS = 512
BLOCK = 128
HALO = 128
CHANNELS = 2048
TILES = 64


def pair_tables(key):
    device_count = TILES // TILE_SLOTS
    per_device = TILE_SLOTS * BLOCK
    base_key = jax.random.fold_in(key, 7)
    first_key, offset_key, count_key, full_key = jax.random.split(base_key, 4)
    own_offset = jax.random.randint(first_key, (device_count, per_device), 0, CH_DEV)
    reach_chan = jax.random.randint(offset_key, (device_count, per_device), -HALO, HALO + 1)
    own_offset = own_offset.at[:, 0].set(0).at[:, 1].set(CH_DEV - 1)
    reach_chan = reach_chan.at[:, 0].set(-HALO).at[:, 1].set(HALO)
    device_rows = jnp.arange(device_count, dtype=jnp.int32)[:, None]
    first_chan = device_rows * CH_DEV + own_offset
    second_chan = first_chan + reach_chan
    outside = (second_chan < 0) | (second_chan >= CHANNELS)
    second_chan = jnp.where(outside, first_chan - reach_chan, second_chan)
    live_count = jax.random.randint(count_key, (device_count,), BLOCK, per_device * 3 // 4 + 1)
    full_device = jax.random.randint(full_key, (), 0, device_count)
    live_count = jnp.where(jnp.arange(device_count) == full_device, per_device, live_count)
    live_mask = (jnp.arange(per_device)[None, :] < live_count[:, None]).astype(jnp.int32)
    pair_table = jnp.stack([first_chan, second_chan], axis=-1).reshape(TILES, BLOCK, 2)
    return (pair_table.astype(jnp.int32), live_mask.reshape(TILES, BLOCK))


def draw_pair_channels(key, part):
    return pair_tables(key)[0]


def draw_pair_live(key, part):
    return pair_tables(key)[1]


def draw_spectra(key, part):
    key_list = jax.random.split(jax.random.fold_in(key, 11), 5)
    position = jnp.arange(CHANNELS, dtype=jnp.float32) / (CHANNELS - 1)
    coupling = (1.0 + 2.0 * position) * jnp.exp(jax.random.uniform(key_list[0], (CHANNELS,), minval=-0.5, maxval=0.5))
    bin_scale = jnp.exp(jax.random.uniform(key_list[1], (FREQ,), minval=math.log(0.3), maxval=math.log(3.0)))
    shape_all = (CHANNELS, WIN, 2, FREQ)
    row_scale = jnp.exp(jax.random.uniform(key_list[2], (CHANNELS,), minval=math.log(0.3), maxval=math.log(3.0)))
    common = jnp.clip(jax.random.normal(key_list[3], (WIN, 2, FREQ)), -5.0, 5.0)
    noise_part = jnp.clip(jax.random.normal(key_list[4], shape_all), -5.0, 5.0)
    values = coupling[:, None, None, None] * common[None] + 0.6 * row_scale[:, None, None, None] * noise_part
    return (values * bin_scale).astype(jnp.bfloat16)


def setup_inputs(seed: int = 0, part: int = 0) -> dict:
    key_of = jax.random.split(jax.random.key(seed), 4)
    part_keys = jax.random.split(jax.random.fold_in(key_of[3], part), 4)
    spectra = draw_spectra(jax.random.fold_in(jax.random.fold_in(key_of[3], part), 71), part)
    pair_channels = draw_pair_channels(jax.random.fold_in(key_of[3], 71), part)
    pair_live = draw_pair_live(jax.random.fold_in(key_of[3], 71), part)
    return {"spectra": spectra, "pair_channels": pair_channels, "pair_live": pair_live}


def build_table(bin_total, lag_total):
    bin_index = jnp.arange(bin_total, dtype=jnp.int32)[:, None]
    shifts = jnp.arange(lag_total, dtype=jnp.int32)[None, :] - lag_total // 2
    phase_int = jnp.mod(bin_index * shifts, 2 * bin_total)
    angle_rad = phase_int.astype(jnp.float32) * (math.pi / bin_total)
    return jnp.concatenate([jnp.cos(angle_rad), -jnp.sin(angle_rad)], axis=0).astype(jnp.bfloat16)

def whiten(raw_rows, common):
    removed = raw_rows.astype(jnp.float32) - common[None]
    magnitude = jnp.sqrt(removed[:, :, 0] ** 2 + removed[:, :, 1] ** 2)
    row_count, window_count, bin_count = magnitude.shape
    banded = magnitude.reshape(row_count, window_count, bin_count // BAND, BAND)
    band_level = lax.optimization_barrier(jnp.mean(banded, axis=3, keepdims=True)) + 1e-06
    scaled = removed.reshape(row_count, window_count, 2, bin_count // BAND, BAND) / band_level[:, :, None]
    return scaled.reshape(raw_rows.shape).astype(jnp.bfloat16)

def cross_rows(first_rows, second_rows):
    first_f32 = first_rows.astype(jnp.float32)
    second_f32 = second_rows.astype(jnp.float32)
    real_part = lax.optimization_barrier(jnp.sum(first_f32[:, :, 0] * second_f32[:, :, 0] + first_f32[:, :, 1] * second_f32[:, :, 1], axis=1))
    imag_part = lax.optimization_barrier(jnp.sum(first_f32[:, :, 1] * second_f32[:, :, 0] - first_f32[:, :, 0] * second_f32[:, :, 1], axis=1))
    return jnp.concatenate([real_part, imag_part], axis=1).astype(jnp.bfloat16)

def reference(spectra, pair_channels, pair_live):
    common = lax.optimization_barrier(jnp.sum(spectra, axis=0, dtype=jnp.float32)) / CHANNELS
    whitened = whiten(spectra, common)
    lag_matrix = build_table(FREQ, LAGS)
    norm_factor = 1.0 / math.sqrt(FREQ * WIN)

    def one_tile(operands):
        tile_pairs, tile_live = operands
        products = cross_rows(whitened[tile_pairs[:, 0]], whitened[tile_pairs[:, 1]])
        summed = jnp.dot(products, lag_matrix, preferred_element_type=jnp.float32)
        return summed * norm_factor * tile_live.astype(jnp.float32)[:, None]
    return lax.map(one_tile, (pair_channels, pair_live))
```

```python
import functools
import math

import jax
import jax.numpy as jnp
from jax import lax
from jax.experimental import pallas as pl
from jax.experimental.pallas import tpu as pltpu
from jax.sharding import PartitionSpec as P

BAND = 64
LAGS = 512
HALO = 128
CHUNK = 256


def permuted(block, axis):
    count = lax.axis_size(axis)
    forward = [(i, i + 1) for i in range(count - 1)]
    backward = [(target, source) for source, target in forward]
    low = lax.ppermute(block[block.shape[0] - HALO :], axis, forward)
    high = lax.ppermute(block[:HALO], axis, backward)
    return low, high


def phase_table(bins, bin_total):
    shifts = jnp.arange(LAGS, dtype=jnp.int32)[None, :] - LAGS // 2
    phase_int = jnp.mod(bins[:, None] * shifts, 2 * bin_total)
    angle_rad = phase_int.astype(jnp.float32) * (math.pi / bin_total)
    return jnp.cos(angle_rad), jnp.sin(angle_rad)


def kernel(windows, norm_factor, *refs):
    parts = 2 * windows
    raw = [refs[i * parts : (i + 1) * parts] for i in range(3)]
    common_ref, first_ref, second_ref, live_ref, cl_ref, sl_ref, ch_ref, sh_ref = refs[
        3 * parts : 3 * parts + 8
    ]
    out_ref, pick_a, pick_b, white = refs[3 * parts + 8 :]
    step = pl.program_id(0)
    rows, total_rows = raw[1][0].shape[0], white.shape[0]
    pairs = out_ref.shape[0]
    chunk = raw[0][0].shape[1]

    @pl.when(step == 0)
    def _():
        own = lax.broadcasted_iota(jnp.int32, (pairs, rows), 1)
        pick_a[...] = (first_ref[...] == own).astype(jnp.float32).astype(jnp.bfloat16)
        band = lax.broadcasted_iota(jnp.int32, (pairs, total_rows), 1)
        pick_b[...] = (second_ref[...] == band).astype(jnp.float32).astype(jnp.bfloat16)
        out_ref[...] = jnp.zeros_like(out_ref)

    lane_r = lax.broadcasted_iota(jnp.int32, (chunk, chunk), 0) // BAND
    lane_c = lax.broadcasted_iota(jnp.int32, (chunk, chunk), 1) // BAND
    same = (lane_r == lane_c).astype(jnp.float32).astype(jnp.bfloat16)
    start = 0
    for side in range(3):
        count = raw[side][0].shape[0]
        for w in range(windows):
            re = raw[side][2 * w][...].astype(jnp.float32) - common_ref[2 * w : 2 * w + 1, :]
            im = raw[side][2 * w + 1][...].astype(jnp.float32) - common_ref[2 * w + 1 : 2 * w + 2, :]
            mag = jnp.sqrt(re * re + im * im)
            hi = mag.astype(jnp.bfloat16)
            lo = (mag - hi.astype(jnp.float32)).astype(jnp.bfloat16)
            level = jnp.dot(hi, same, preferred_element_type=jnp.float32)
            level += jnp.dot(lo, same, preferred_element_type=jnp.float32)
            scale = 1.0 / (level * (1.0 / BAND) + 1e-06)
            at = 2 * w * chunk
            white[start : start + count, at : at + chunk] = (re * scale).astype(jnp.bfloat16)
            white[start : start + count, at + chunk : at + 2 * chunk] = (im * scale).astype(jnp.bfloat16)
        start += count

    cl, sl, ch, sh = cl_ref[...], sl_ref[...], ch_ref[0], sh_ref[0]
    lag_re = (cl * ch - sl * sh).astype(jnp.bfloat16)
    lag_im = (-(sl * ch + cl * sh)).astype(jnp.bfloat16)
    low_rows = raw[0][0].shape[0]
    tile = 128

    def one(i, carry):
        at = pl.ds(pl.multiple_of(i * tile, tile), tile)
        a = jnp.dot(pick_a[at, :], white[low_rows : low_rows + rows, :], preferred_element_type=jnp.float32)
        b = jnp.dot(pick_b[at, :], white[...], preferred_element_type=jnp.float32)
        cross_re = jnp.zeros((tile, chunk), jnp.float32)
        cross_im = jnp.zeros((tile, chunk), jnp.float32)
        for w in range(windows):
            lo = 2 * w * chunk
            ar, ai = a[:, lo : lo + chunk], a[:, lo + chunk : lo + 2 * chunk]
            br, bi = b[:, lo : lo + chunk], b[:, lo + chunk : lo + 2 * chunk]
            cross_re += ar * br + ai * bi
            cross_im += ai * br - ar * bi
        total = jnp.dot(cross_re.astype(jnp.bfloat16), lag_re, preferred_element_type=jnp.float32)
        total += jnp.dot(cross_im.astype(jnp.bfloat16), lag_im, preferred_element_type=jnp.float32)
        out_ref[at, :] += total
        return carry

    lax.fori_loop(0, pairs // tile, one, 0)

    @pl.when(step == pl.num_programs(0) - 1)
    def _():
        out_ref[...] = out_ref[...] * (norm_factor * live_ref[...])


def body(spectra, pair_channels, pair_live):
    own_rows, windows, _, bins = spectra.shape
    channels = own_rows * lax.axis_size("row")
    first_own = lax.axis_index("row") * own_rows
    flat = spectra.reshape(own_rows, windows * 2 * bins)
    low, high = permuted(flat, "row")
    local_sum = jnp.sum(spectra, axis=0, dtype=jnp.float32)
    common = (lax.psum(local_sum, "row") / channels).reshape(windows * 2, bins)
    steps = bins // CHUNK
    cl, sl = phase_table(jnp.arange(CHUNK, dtype=jnp.int32), bins)
    ch, sh = phase_table(jnp.arange(steps, dtype=jnp.int32) * CHUNK, bins)
    tile_count, tile_pairs = pair_live.shape
    pairs = tile_count * tile_pairs
    index = pair_channels.reshape(pairs, 2)
    first = index[:, 0:1] - first_own
    second = index[:, 1:2] - (first_own - HALO)
    live = pair_live.reshape(pairs, 1).astype(jnp.float32)
    parts = 2 * windows

    def strips(count):
        return [pl.BlockSpec((count, CHUNK), lambda c, k=k: (0, k * steps + c)) for k in range(parts)]

    def whole(shape):
        return pl.BlockSpec(shape, lambda c: (0, 0))

    result = pl.pallas_call(
        functools.partial(kernel, windows, 1.0 / math.sqrt(bins * windows)),
        grid=(steps,),
        out_shape=jax.ShapeDtypeStruct((pairs, LAGS), jnp.float32),
        in_specs=strips(HALO) + strips(own_rows) + strips(HALO) + [
            pl.BlockSpec((parts, CHUNK), lambda c: (0, c)),
            whole((pairs, 1)), whole((pairs, 1)), whole((pairs, 1)),
            whole((CHUNK, LAGS)), whole((CHUNK, LAGS)),
            pl.BlockSpec((1, 1, LAGS), lambda c: (c, 0, 0)),
            pl.BlockSpec((1, 1, LAGS), lambda c: (c, 0, 0)),
        ],
        out_specs=whole((pairs, LAGS)),
        scratch_shapes=[
            pltpu.VMEM((pairs, own_rows), jnp.bfloat16),
            pltpu.VMEM((pairs, own_rows + 2 * HALO), jnp.bfloat16),
            pltpu.VMEM((own_rows + 2 * HALO, parts * CHUNK), jnp.bfloat16),
        ],
    )(*([low] * parts + [flat] * parts + [high] * parts), common, first, second, live, cl, sl,
      ch[:, None, :], sh[:, None, :])
    return result.reshape(tile_count, tile_pairs, LAGS)


def solution(mesh):
    placed = (P(("day", "row"), None, None, None), P("row", None, None), P("row", None))
    return jax.shard_map(
        body, mesh=mesh, in_specs=placed, out_specs=P(("day", "row"), None, None), check_vma=False
    )
```

```python
import functools
import math

import jax
import jax.numpy as jnp
from jax import lax
from jax.experimental import pallas as pl
from jax.experimental.pallas import tpu as pltpu
from jax.sharding import PartitionSpec as P

BAND = 64
LAGS = 512
CHUNK = 256
PRE = 4


def phase_table(bins, bin_total):
    shifts = jnp.arange(LAGS, dtype=jnp.int32)[None, :] - LAGS // 2
    phase_int = jnp.mod(bins[:, None] * shifts, 2 * bin_total)
    angle_rad = phase_int.astype(jnp.float32) * (math.pi / bin_total)
    return jnp.cos(angle_rad), jnp.sin(angle_rad)


MESH = pl.DeviceIdType.MESH


def kernel(count, windows, norm_factor, own_hbm, first_ref, second_ref, live_ref, cl_ref, sl_ref, ch_ref, sh_ref,
           out_ref, own, halo, pick_a, pick_b, white, sums, heard,
           load_sem, send_sem, recv_sem, sum_send, sum_recv):
    parts = 2 * windows
    steps, rows, width = own.shape
    chunk = width // parts
    bins = steps * chunk
    pairs = out_ref.shape[0]
    me = lax.axis_index("row")
    rounds = count.bit_length() - 1
    channels = count * rows

    def load(c, k):
        return pltpu.make_async_copy(
            own_hbm.at[:, pl.ds(pl.multiple_of(k * bins + c * chunk, chunk), chunk)],
            own.at[c, :, pl.ds(k * chunk, chunk)], load_sem.at[c, k])

    def send(side, c, target):
        return pltpu.make_async_remote_copy(
            src_ref=own.at[c], dst_ref=halo.at[side, c], send_sem=send_sem.at[side, c],
            recv_sem=recv_sem.at[side, c], device_id={"row": target}, device_id_type=MESH)

    def send_chunk(c):
        @pl.when(me < count - 1)
        def _():
            send(0, c, me + 1).start()

        @pl.when(me > 0)
        def _():
            send(1, c, me - 1).start()

    for k in range(parts):
        @pl.loop(0, steps)
        def _(c, k=k):
            load(c, k).start()

    barrier = pltpu.get_barrier_semaphore()
    partners = [me ^ (1 << r) for r in range(rounds)]
    for partner in partners:
        pl.semaphore_signal(barrier, inc=1, device_id={"row": partner}, device_id_type=MESH)

    other = lax.rem(me + 2 * lax.rem(me, 2) - 1 + count, count)
    pl.semaphore_signal(barrier, inc=1, device_id={"row": other}, device_id_type=MESH)

    own_index = lax.broadcasted_iota(jnp.int32, (pairs, rows), 1)
    pick_a[...] = (first_ref[...] == own_index).astype(jnp.float32).astype(jnp.bfloat16)
    band = lax.broadcasted_iota(jnp.int32, (pairs, white.shape[0]), 1)
    pick_b[...] = (second_ref[...] == band).astype(jnp.float32).astype(jnp.bfloat16)
    out_ref[...] = jnp.zeros_like(out_ref)

    @pl.when(me == 0)
    def _():
        @pl.loop(0, steps)
        def _(c):
            halo[0, c] = jnp.zeros((rows, width), jnp.bfloat16)

    @pl.when(me == count - 1)
    def _():
        @pl.loop(0, steps)
        def _(c):
            halo[1, c] = jnp.zeros((rows, width), jnp.bfloat16)

    @pl.loop(0, steps)
    def _(c):
        for k in range(parts):
            load(c, k).wait()
            block = own[c, :, k * chunk : (k + 1) * chunk].astype(jnp.float32)
            sums[0, c, k : k + 1, :] = jnp.sum(block, axis=0, keepdims=True)

    pl.semaphore_wait(barrier, rounds + 1)

    copies = []
    for r in range(rounds):
        copy = pltpu.make_async_remote_copy(
            src_ref=sums.at[r], dst_ref=heard.at[r], send_sem=sum_send.at[r], recv_sem=sum_recv.at[r],
            device_id={"row": partners[r]}, device_id_type=MESH)
        copy.start()
        copies.append(copy)
        if r < min(PRE, steps):
            send_chunk(r)
        copy.wait_recv()
        sums[r + 1] = sums[r] + heard[r]

    @pl.loop(min(PRE, rounds, steps), steps)
    def _(c):
        send_chunk(c)

    lane_r = lax.broadcasted_iota(jnp.int32, (chunk, chunk), 0) // BAND
    lane_c = lax.broadcasted_iota(jnp.int32, (chunk, chunk), 1) // BAND
    same = (lane_r == lane_c).astype(jnp.float32).astype(jnp.bfloat16)

    def whiten(c, source, start):
        for w in range(windows):
            at = 2 * w * chunk
            common = sums[rounds, c] * (1.0 / channels)
            re = source[:, at : at + chunk].astype(jnp.float32) - common[2 * w : 2 * w + 1, :]
            im = source[:, at + chunk : at + 2 * chunk].astype(jnp.float32) - common[2 * w + 1 : 2 * w + 2, :]
            mag = jnp.sqrt(re * re + im * im)
            hi = mag.astype(jnp.bfloat16)
            lo = (mag - hi.astype(jnp.float32)).astype(jnp.bfloat16)
            level = jnp.dot(hi, same, preferred_element_type=jnp.float32)
            level += jnp.dot(lo, same, preferred_element_type=jnp.float32)
            scale = 1.0 / (level * (1.0 / BAND) + 1e-06)
            white[start : start + rows, at : at + chunk] = (re * scale).astype(jnp.bfloat16)
            white[start : start + rows, at + chunk : at + 2 * chunk] = (im * scale).astype(jnp.bfloat16)

    @pl.loop(0, steps)
    def _(c):
        whiten(c, own.at[c], rows)

        @pl.when(me > 0)
        def _():
            send(0, c, me - 1).wait_recv()

        whiten(c, halo.at[0, c], 0)

        @pl.when(me < count - 1)
        def _():
            send(1, c, me + 1).wait_recv()

        whiten(c, halo.at[1, c], 2 * rows)
        cl, sl, ch, sh = cl_ref[...], sl_ref[...], ch_ref[c], sh_ref[c]
        lag_re = (cl * ch - sl * sh).astype(jnp.bfloat16)
        lag_im = (-(sl * ch + cl * sh)).astype(jnp.bfloat16)
        tile = 128

        @pl.loop(0, pairs // tile)
        def _(i):
            at = pl.ds(pl.multiple_of(i * tile, tile), tile)
            a = jnp.dot(pick_a[at, :], white[rows : 2 * rows, :], preferred_element_type=jnp.float32)
            b = jnp.dot(pick_b[at, :], white[...], preferred_element_type=jnp.float32)
            cross_re = jnp.zeros((tile, chunk), jnp.float32)
            cross_im = jnp.zeros((tile, chunk), jnp.float32)
            for w in range(windows):
                lo = 2 * w * chunk
                ar, ai = a[:, lo : lo + chunk], a[:, lo + chunk : lo + 2 * chunk]
                br, bi = b[:, lo : lo + chunk], b[:, lo + chunk : lo + 2 * chunk]
                cross_re += ar * br + ai * bi
                cross_im += ai * br - ar * bi
            total = jnp.dot(cross_re.astype(jnp.bfloat16), lag_re, preferred_element_type=jnp.float32)
            total += jnp.dot(cross_im.astype(jnp.bfloat16), lag_im, preferred_element_type=jnp.float32)
            out_ref[at, :] += total

    out_ref[...] = out_ref[...] * (norm_factor * live_ref[...])
    for copy in copies:
        copy.wait_send()

    @pl.loop(0, steps)
    def _(c):
        @pl.when(me < count - 1)
        def _():
            send(0, c, me + 1).wait_send()

        @pl.when(me > 0)
        def _():
            send(1, c, me - 1).wait_send()


def body(spectra, pair_channels, pair_live):
    rows, windows, _, bins = spectra.shape
    count = lax.axis_size("row")
    first_own = lax.axis_index("row") * rows
    parts = 2 * windows
    flat = spectra.reshape(rows, parts * bins)
    steps = bins // CHUNK
    cl, sl = phase_table(jnp.arange(CHUNK, dtype=jnp.int32), bins)
    ch, sh = phase_table(jnp.arange(steps, dtype=jnp.int32) * CHUNK, bins)
    tile_count, tile_pairs = pair_live.shape
    pairs = tile_count * tile_pairs
    index = pair_channels.reshape(pairs, 2)
    first = index[:, 0:1] - first_own
    second = index[:, 1:2] - (first_own - rows)
    live = pair_live.reshape(pairs, 1).astype(jnp.float32)
    rounds = count.bit_length() - 1
    vmem = pl.BlockSpec(memory_space=pltpu.VMEM)
    result = pl.pallas_call(
        functools.partial(kernel, count, windows, 1.0 / math.sqrt(bins * windows)),
        out_shape=jax.ShapeDtypeStruct((pairs, LAGS), jnp.float32),
        in_specs=[pl.BlockSpec(memory_space=pl.ANY)] + [vmem] * 7,
        out_specs=vmem,
        scratch_shapes=[
            pltpu.VMEM((steps, rows, parts * CHUNK), jnp.bfloat16),
            pltpu.VMEM((2, steps, rows, parts * CHUNK), jnp.bfloat16),
            pltpu.VMEM((pairs, rows), jnp.bfloat16),
            pltpu.VMEM((pairs, 3 * rows), jnp.bfloat16),
            pltpu.VMEM((3 * rows, parts * CHUNK), jnp.bfloat16),
            pltpu.VMEM((rounds + 1, steps, parts, CHUNK), jnp.float32),
            pltpu.VMEM((rounds, steps, parts, CHUNK), jnp.float32),
            pltpu.SemaphoreType.DMA((steps, parts)),
            pltpu.SemaphoreType.DMA((2, steps)),
            pltpu.SemaphoreType.DMA((2, steps)),
            pltpu.SemaphoreType.DMA((rounds,)),
            pltpu.SemaphoreType.DMA((rounds,)),
        ],
        compiler_params=pltpu.CompilerParams(
            collective_id=0, has_side_effects=True, vmem_limit_bytes=60 * 2**20),
    )(flat, first, second, live, cl, sl, ch[:, None, :], sh[:, None, :])
    return result.reshape(tile_count, tile_pairs, LAGS)


def solution(mesh):
    placed = (P(("day", "row"), None, None, None), P("row", None, None), P("row", None))
    return jax.shard_map(
        body, mesh=mesh, in_specs=placed, out_specs=P(("day", "row"), None, None), check_vma=False
    )
```

```python
import functools
import math

import jax
import jax.numpy as jnp
from jax import lax
from jax.experimental import pallas as pl
from jax.experimental.pallas import tpu as pltpu
from jax.sharding import PartitionSpec as P

BAND = 64
LAGS = 512
CHUNK = 256
TILE = 256


MESH = pl.DeviceIdType.MESH


def kernel(count, windows, norm_factor, own_hbm, pack_ref, out_ref, own, halo, pack, pick_a, pick_b, white,
           base, acc, back_out, back_in, sums, heard,
           load_sem, send_sem, recv_sem, sum_send, sum_recv, pack_send, pack_recv, back_send, back_recv):
    parts = 2 * windows
    steps, rows, width = own.shape
    half = steps // 2
    chunk = width // parts
    bins = steps * chunk
    pairs = out_ref.shape[0]
    me = lax.axis_index("row")
    first_own = me * rows
    rounds = count.bit_length() - 1
    channels = count * rows
    has_left, has_right = me > 0, me < count - 1

    def load(c, k):
        return pltpu.make_async_copy(
            own_hbm.at[:, pl.ds(pl.multiple_of(k * bins + c * chunk, chunk), chunk)],
            own.at[c, :, pl.ds(k * chunk, chunk)], load_sem.at[c, k])

    def remote(src, dst, sent, got, target):
        return pltpu.make_async_remote_copy(
            src_ref=src, dst_ref=dst, send_sem=sent, recv_sem=got,
            device_id={"row": target}, device_id_type=MESH)

    def send(c, target):
        return remote(own.at[c], halo.at[c], send_sem.at[c], recv_sem.at[c], target)

    def send_pack(side, target):
        return remote(pack_ref, pack.at[side], pack_send.at[side], pack_recv.at[side], target)

    def send_back(side, target):
        return remote(back_out.at[side], back_in.at[side], back_send.at[side], back_recv.at[side], target)

    for k in range(parts):
        @pl.loop(0, steps)
        def _(c, k=k):
            load(c, k).start()

    barrier = pltpu.get_barrier_semaphore()
    partners = [me ^ (1 << r) for r in range(rounds)]
    for partner in partners:
        pl.semaphore_signal(barrier, inc=1, device_id={"row": partner}, device_id_type=MESH)
    other = lax.rem(me + 2 * lax.rem(me, 2) - 1 + count, count)
    pl.semaphore_signal(barrier, inc=1, device_id={"row": other}, device_id_type=MESH)

    acc[...] = jnp.zeros_like(acc)

    @pl.when(jnp.logical_not(has_left))
    def _():
        pack[0] = jnp.zeros(pack.shape[1:], jnp.int32)

        @pl.loop(0, half)
        def _(c):
            halo[c] = jnp.zeros((rows, width), jnp.bfloat16)

    @pl.when(jnp.logical_not(has_right))
    def _():
        pack[1] = jnp.zeros(pack.shape[1:], jnp.int32)

        @pl.loop(half, steps)
        def _(c):
            halo[c] = jnp.zeros((rows, width), jnp.bfloat16)

    @pl.loop(0, steps)
    def _(c):
        for k in range(parts):
            load(c, k).wait()
            block = own[c, :, k * chunk : (k + 1) * chunk].astype(jnp.float32)
            sums[0, c, k : k + 1, :] = jnp.sum(block, axis=0, keepdims=True)

    pl.semaphore_wait(barrier, rounds + 1)

    def add_up(r):
        copy = remote(sums.at[r], heard.at[r], sum_send.at[r], sum_recv.at[r], partners[r])
        copy.start()
        return copy

    copies = [add_up(0)]

    @pl.when(has_right)
    def _():
        send_pack(0, me + 1).start()

    @pl.when(has_left)
    def _():
        send_pack(1, me - 1).start()

    for r in range(rounds):
        if r == 0:
            shifts = lax.broadcasted_iota(jnp.int32, (chunk, LAGS), 1) + (2 * bins - LAGS // 2)
            phase = lax.rem(lax.broadcasted_iota(jnp.int32, (chunk, LAGS), 0) * shifts, 2 * bins)
            angle = phase.astype(jnp.float32) * (math.pi / bins)
            base[0] = jnp.cos(angle)
            base[1] = jnp.sin(angle)
        if r == 1:
            @pl.when(has_left)
            def _():
                send_pack(0, me - 1).wait_recv()

            @pl.when(has_right)
            def _():
                send_pack(1, me + 1).wait_recv()

            row = lax.broadcasted_iota(jnp.int32, (2 * rows, pairs), 0)
            for side in range(2):
                beside = first_own - rows if side == 0 else first_own + rows

                def pick(index, near):
                    inside = (index >= first_own) & (index < first_own + rows)
                    mine = jnp.where(inside, index - first_own + rows, -1)
                    if not near:
                        return mine
                    across = (index >= beside) & (index < beside + rows)
                    return jnp.where(across, index - beside, mine)

                for group in range(2):
                    table = pack_ref[...] if group == side_own(side) else pack[side]
                    first, second, live = table[0:1], table[1:2], table[2:3].astype(jnp.float32)
                    near = group == side_own(side)
                    at = slice(group * pairs, (group + 1) * pairs)
                    a_row = pick(first, True)
                    b_row = pick(second, near)
                    hot_a = (row == a_row).astype(jnp.float32) * live
                    hot_b = (row == b_row).astype(jnp.float32)
                    pick_a[side, at, :] = jnp.transpose(hot_a).astype(jnp.bfloat16)
                    pick_b[side, at, :] = jnp.transpose(hot_b).astype(jnp.bfloat16)
        copies[r].wait_recv()
        sums[r + 1] = sums[r] + heard[r]
        if r + 1 < rounds:
            copies.append(add_up(r + 1))

    @pl.when(has_right)
    def _():
        @pl.loop(0, half)
        def _(c):
            send(c, me + 1).start()

    lane_r = lax.broadcasted_iota(jnp.int32, (chunk, chunk), 0) // BAND
    lane_c = lax.broadcasted_iota(jnp.int32, (chunk, chunk), 1) // BAND
    same = (lane_r == lane_c).astype(jnp.float32).astype(jnp.bfloat16)

    def whiten(c, source, start):
        common = sums[rounds, c] * (1.0 / channels)
        for w in range(windows):
            at = 2 * w * chunk
            re = source[:, at : at + chunk].astype(jnp.float32) - common[2 * w : 2 * w + 1, :]
            im = source[:, at + chunk : at + 2 * chunk].astype(jnp.float32) - common[2 * w + 1 : 2 * w + 2, :]
            power = re * re + im * im
            mag = power * lax.rsqrt(jnp.maximum(power, 1e-30))
            hi = mag.astype(jnp.bfloat16)
            lo = (mag - hi.astype(jnp.float32)).astype(jnp.bfloat16)
            level = jnp.dot(hi, same, preferred_element_type=jnp.float32)
            level += jnp.dot(lo, same, preferred_element_type=jnp.float32)
            scale = 1.0 / (level * (1.0 / BAND) + 1e-06)
            white[start : start + rows, at : at + chunk] = (re * scale).astype(jnp.bfloat16)
            white[start : start + rows, at + chunk : at + 2 * chunk] = (im * scale).astype(jnp.bfloat16)

    shift_row = lax.broadcasted_iota(jnp.int32, (8, LAGS), 1) + (2 * bins - LAGS // 2)

    def correlate(side, c):
        turn = lax.rem(lax.rem(c * shift_row, 2 * bins) * chunk, 2 * bins).astype(jnp.float32) * (math.pi / bins)
        ch, sh = jnp.cos(turn)[0:1], jnp.sin(turn)[0:1]
        lag_re = (base[0] * ch - base[1] * sh).astype(jnp.bfloat16)
        lag_im = (-(base[1] * ch + base[0] * sh)).astype(jnp.bfloat16)
        tile = TILE

        @pl.loop(0, 2 * pairs // tile)
        def _(i):
            at = pl.ds(pl.multiple_of(i * tile, tile), tile)
            to = pl.ds(pl.multiple_of(side * pairs + i * tile, tile), tile)
            cross_re = jnp.zeros((tile, chunk), jnp.float32)
            cross_im = jnp.zeros((tile, chunk), jnp.float32)
            for w in range(windows):
                lo = 2 * w * chunk
                a = jnp.dot(pick_a[side, at, :], white[:, lo : lo + 2 * chunk], preferred_element_type=jnp.float32)
                b = jnp.dot(pick_b[side, at, :], white[:, lo : lo + 2 * chunk], preferred_element_type=jnp.float32)
                ar, ai, br, bi = a[:, :chunk], a[:, chunk:], b[:, :chunk], b[:, chunk:]
                cross_re += ar * br + ai * bi
                cross_im += ai * br - ar * bi
            total = jnp.dot(cross_re.astype(jnp.bfloat16), lag_re, preferred_element_type=jnp.float32)
            total += jnp.dot(cross_im.astype(jnp.bfloat16), lag_im, preferred_element_type=jnp.float32)
            acc[to, :] += total

    @pl.loop(0, half)
    def _(c):
        @pl.when(has_left)
        def _():
            send(half + c, me - 1).start()

        whiten(c, own.at[c], rows)

        @pl.when(has_left)
        def _():
            send(c, me - 1).wait_recv()

        whiten(c, halo.at[c], 0)
        correlate(0, c)

    back_out[0] = acc[0:pairs, :].astype(jnp.bfloat16)

    @pl.when(has_left)
    def _():
        send_back(0, me - 1).start()

    @pl.loop(half, steps)
    def _(c):
        whiten(c, own.at[c], rows)

        @pl.when(has_right)
        def _():
            send(c, me + 1).wait_recv()

        whiten(c, halo.at[c], 0)
        correlate(1, c)

    back_out[1] = acc[2 * pairs : 3 * pairs, :].astype(jnp.bfloat16)

    @pl.when(has_right)
    def _():
        send_back(1, me + 1).start()
        send_back(0, me + 1).wait_recv()
        acc[pairs : 2 * pairs, :] += back_in[0].astype(jnp.float32)

    @pl.when(has_left)
    def _():
        send_back(1, me - 1).wait_recv()
        acc[pairs : 2 * pairs, :] += back_in[1].astype(jnp.float32)

    out_ref[...] = acc[pairs : 2 * pairs, :] * norm_factor
    for copy in copies:
        copy.wait_send()

    @pl.when(has_right)
    def _():
        send_pack(0, me + 1).wait_send()
        send_back(1, me + 1).wait_send()

        @pl.loop(0, half)
        def _(c):
            send(c, me + 1).wait_send()

    @pl.when(has_left)
    def _():
        send_pack(1, me - 1).wait_send()
        send_back(0, me - 1).wait_send()

        @pl.loop(half, steps)
        def _(c):
            send(c, me - 1).wait_send()


def side_own(side):
    return 1 - side


def body(spectra, pair_channels, pair_live):
    rows, windows, _, bins = spectra.shape
    count = lax.axis_size("row")
    parts = 2 * windows
    flat = spectra.reshape(rows, parts * bins)
    steps = bins // CHUNK
    tile_count, tile_pairs = pair_live.shape
    pairs = tile_count * tile_pairs
    index = jnp.transpose(pair_channels, (2, 0, 1)).reshape(2, pairs)
    packed = jnp.concatenate([index, pair_live.reshape(1, pairs)], axis=0)
    rounds = count.bit_length() - 1
    vmem = pl.BlockSpec(memory_space=pltpu.VMEM)
    dma = pltpu.SemaphoreType.DMA
    result = pl.pallas_call(
        functools.partial(kernel, count, windows, 1.0 / math.sqrt(bins * windows)),
        out_shape=jax.ShapeDtypeStruct((pairs, LAGS), jnp.float32),
        in_specs=[pl.BlockSpec(memory_space=pl.ANY), vmem],
        out_specs=vmem,
        scratch_shapes=[
            pltpu.VMEM((steps, rows, parts * CHUNK), jnp.bfloat16),
            pltpu.VMEM((steps, rows, parts * CHUNK), jnp.bfloat16),
            pltpu.VMEM((2, 3, pairs), jnp.int32),
            pltpu.VMEM((2, 2 * pairs, 2 * rows), jnp.bfloat16),
            pltpu.VMEM((2, 2 * pairs, 2 * rows), jnp.bfloat16),
            pltpu.VMEM((2 * rows, parts * CHUNK), jnp.bfloat16),
            pltpu.VMEM((2, CHUNK, LAGS), jnp.float32),
            pltpu.VMEM((3 * pairs, LAGS), jnp.float32),
            pltpu.VMEM((2, pairs, LAGS), jnp.bfloat16),
            pltpu.VMEM((2, pairs, LAGS), jnp.bfloat16),
            pltpu.VMEM((rounds + 1, steps, parts, CHUNK), jnp.float32),
            pltpu.VMEM((rounds, steps, parts, CHUNK), jnp.float32),
            dma((steps, parts)), dma((steps,)), dma((steps,)), dma((rounds,)), dma((rounds,)),
            dma((2,)), dma((2,)), dma((2,)), dma((2,)),
        ],
        compiler_params=pltpu.CompilerParams(
            collective_id=0, has_side_effects=True, vmem_limit_bytes=60 * 2**20),
    )(flat, packed)
    return result.reshape(tile_count, tile_pairs, LAGS)


def solution(mesh):
    placed = (P(("day", "row"), None, None, None), P("row", None, None), P("row", None))
    return jax.shard_map(
        body, mesh=mesh, in_specs=placed, out_specs=P(("day", "row"), None, None), check_vma=False
    )
```

```python
import functools
import math

import jax
import jax.numpy as jnp
from jax import lax
from jax.experimental import pallas as pl
from jax.experimental.pallas import tpu as pltpu
from jax.sharding import PartitionSpec as P

BAND = 64
LAGS = 512
CHUNK = 256
TILE = 512


MESH = pl.DeviceIdType.MESH


def kernel(count, windows, norm_factor, own_hbm, pack_ref, out_ref, own, halo, pack, pick_a, pick_b, white,
           base, acc, back_out, back_in, sums, heard,
           load_sem, send_sem, recv_sem, sum_send, sum_recv, pack_send, pack_recv, back_send, back_recv):
    parts = 2 * windows
    steps, rows, width = own.shape
    half = steps // 2
    chunk = width // parts
    bins = steps * chunk
    pairs = out_ref.shape[0]
    me = lax.axis_index("row")
    first_own = me * rows
    rounds = count.bit_length() - 1
    channels = count * rows
    has_left, has_right = me > 0, me < count - 1

    def load(c, k):
        return pltpu.make_async_copy(
            own_hbm.at[:, pl.ds(pl.multiple_of(k * bins + c * chunk, chunk), chunk)],
            own.at[c, :, pl.ds(k * chunk, chunk)], load_sem.at[c, k])

    def remote(src, dst, sent, got, target):
        return pltpu.make_async_remote_copy(
            src_ref=src, dst_ref=dst, send_sem=sent, recv_sem=got,
            device_id={"row": target}, device_id_type=MESH)

    def send(c, target):
        return remote(own.at[c], halo.at[c], send_sem.at[c], recv_sem.at[c], target)

    def send_pack(side, target):
        return remote(pack_ref, pack.at[side], pack_send.at[side], pack_recv.at[side], target)

    def send_back(side, target):
        return remote(back_out.at[side], back_in.at[side], back_send.at[side], back_recv.at[side], target)

    for k in range(parts):
        @pl.loop(0, steps)
        def _(c, k=k):
            load(c, k).start()

    barrier = pltpu.get_barrier_semaphore()
    partners = [me ^ (1 << r) for r in range(rounds)]
    for partner in partners:
        pl.semaphore_signal(barrier, inc=1, device_id={"row": partner}, device_id_type=MESH)
    other = lax.rem(me + 2 * lax.rem(me, 2) - 1 + count, count)
    pl.semaphore_signal(barrier, inc=1, device_id={"row": other}, device_id_type=MESH)

    acc[...] = jnp.zeros_like(acc)

    @pl.when(jnp.logical_not(has_left))
    def _():
        pack[0] = jnp.zeros(pack.shape[1:], jnp.int32)

        @pl.loop(0, half)
        def _(c):
            halo[c] = jnp.zeros((rows, width), jnp.bfloat16)

    @pl.when(jnp.logical_not(has_right))
    def _():
        pack[1] = jnp.zeros(pack.shape[1:], jnp.int32)

        @pl.loop(half, steps)
        def _(c):
            halo[c] = jnp.zeros((rows, width), jnp.bfloat16)

    @pl.loop(0, steps)
    def _(c):
        for k in range(parts):
            load(c, k).wait()
            block = own[c, :, k * chunk : (k + 1) * chunk].astype(jnp.float32)
            sums[0, c, k : k + 1, :] = jnp.sum(block, axis=0, keepdims=True)

    pl.semaphore_wait(barrier, rounds + 1)

    def add_up(r):
        copy = remote(sums.at[r], heard.at[r], sum_send.at[r], sum_recv.at[r], partners[r])
        copy.start()
        return copy

    copies = [add_up(0)]

    @pl.when(has_right)
    def _():
        send_pack(0, me + 1).start()

    @pl.when(has_left)
    def _():
        send_pack(1, me - 1).start()

    for r in range(rounds):
        if r == 0:
            shifts = lax.broadcasted_iota(jnp.int32, (chunk, LAGS), 1) + (2 * bins - LAGS // 2)
            phase = lax.rem(lax.broadcasted_iota(jnp.int32, (chunk, LAGS), 0) * shifts, 2 * bins)
            angle = phase.astype(jnp.float32) * (math.pi / bins)
            base[0] = jnp.cos(angle)
            base[1] = jnp.sin(angle)
        if r == 1:
            @pl.when(has_left)
            def _():
                send_pack(0, me - 1).wait_recv()

            @pl.when(has_right)
            def _():
                send_pack(1, me + 1).wait_recv()

            row = lax.broadcasted_iota(jnp.int32, (2 * rows, pairs), 0)
            for side in range(2):
                beside = first_own - rows if side == 0 else first_own + rows

                def pick(index, near):
                    inside = (index >= first_own) & (index < first_own + rows)
                    mine = jnp.where(inside, index - first_own + rows, -1)
                    if not near:
                        return mine
                    across = (index >= beside) & (index < beside + rows)
                    return jnp.where(across, index - beside, mine)

                for group in range(2):
                    table = pack_ref[...] if group == side_own(side) else pack[side]
                    first, second, live = table[0:1], table[1:2], table[2:3].astype(jnp.float32)
                    near = group == side_own(side)
                    at = slice(group * pairs, (group + 1) * pairs)
                    a_row = pick(first, True)
                    b_row = pick(second, near)
                    hot_a = (row == a_row).astype(jnp.float32) * live
                    hot_b = (row == b_row).astype(jnp.float32)
                    pick_a[side, at, :] = jnp.transpose(hot_a).astype(jnp.bfloat16)
                    pick_b[side, at, :] = jnp.transpose(hot_b).astype(jnp.bfloat16)
        copies[r].wait_recv()
        sums[r + 1] = sums[r] + heard[r]
        if r + 1 < rounds:
            copies.append(add_up(r + 1))

    @pl.when(has_right)
    def _():
        @pl.loop(0, half)
        def _(c):
            send(c, me + 1).start()

    lane_r = lax.broadcasted_iota(jnp.int32, (chunk, chunk), 0) // BAND
    lane_c = lax.broadcasted_iota(jnp.int32, (chunk, chunk), 1) // BAND
    same = (lane_r == lane_c).astype(jnp.float32).astype(jnp.bfloat16)

    def whiten(c, source, start):
        common = sums[rounds, c] * (1.0 / channels)
        for w in range(windows):
            at = 2 * w * chunk
            re = source[:, at : at + chunk].astype(jnp.float32) - common[2 * w : 2 * w + 1, :]
            im = source[:, at + chunk : at + 2 * chunk].astype(jnp.float32) - common[2 * w + 1 : 2 * w + 2, :]
            power = re * re + im * im
            mag = power * lax.rsqrt(jnp.maximum(power, 1e-30))
            hi = mag.astype(jnp.bfloat16)
            lo = (mag - hi.astype(jnp.float32)).astype(jnp.bfloat16)
            level = jnp.dot(hi, same, preferred_element_type=jnp.float32)
            level += jnp.dot(lo, same, preferred_element_type=jnp.float32)
            scale = 1.0 / (level * (1.0 / BAND) + 1e-06)
            white[start : start + rows, at : at + chunk] = (re * scale).astype(jnp.bfloat16)
            white[start : start + rows, at + chunk : at + 2 * chunk] = (im * scale).astype(jnp.bfloat16)

    shift_row = lax.broadcasted_iota(jnp.int32, (8, LAGS), 1) + (2 * bins - LAGS // 2)

    def correlate(side, c):
        turn = lax.rem(lax.rem(c * shift_row, 2 * bins) * chunk, 2 * bins).astype(jnp.float32) * (math.pi / bins)
        ch, sh = jnp.cos(turn)[0:1], jnp.sin(turn)[0:1]
        lag_re = (base[0] * ch - base[1] * sh).astype(jnp.bfloat16)
        lag_im = (-(base[1] * ch + base[0] * sh)).astype(jnp.bfloat16)
        tile = TILE

        @pl.loop(0, 2 * pairs // tile)
        def _(i):
            at = pl.ds(pl.multiple_of(i * tile, tile), tile)
            to = pl.ds(pl.multiple_of(side * pairs + i * tile, tile), tile)
            cross_re = jnp.zeros((tile, chunk), jnp.float32)
            cross_im = jnp.zeros((tile, chunk), jnp.float32)
            for w in range(windows):
                lo = 2 * w * chunk
                a = jnp.dot(pick_a[side, at, :], white[:, lo : lo + 2 * chunk], preferred_element_type=jnp.float32)
                b = jnp.dot(pick_b[side, at, :], white[:, lo : lo + 2 * chunk], preferred_element_type=jnp.float32)
                ar, ai, br, bi = a[:, :chunk], a[:, chunk:], b[:, :chunk], b[:, chunk:]
                cross_re += ar * br + ai * bi
                cross_im += ai * br - ar * bi
            total = jnp.dot(cross_re.astype(jnp.bfloat16), lag_re, preferred_element_type=jnp.float32)
            total += jnp.dot(cross_im.astype(jnp.bfloat16), lag_im, preferred_element_type=jnp.float32)
            acc[to, :] += total

    @pl.loop(0, half)
    def _(c):
        @pl.when(has_left & (c >= half // 2))
        def _():
            send(2 * c, me - 1).start()
            send(2 * c + 1, me - 1).start()

        whiten(c, own.at[c], rows)

        @pl.when(has_left)
        def _():
            send(c, me - 1).wait_recv()

        whiten(c, halo.at[c], 0)
        correlate(0, c)

    back_out[0] = acc[0:pairs, :].astype(jnp.bfloat16)

    @pl.when(has_left)
    def _():
        send_back(0, me - 1).start()

    @pl.loop(half, steps)
    def _(c):
        whiten(c, own.at[c], rows)

        @pl.when(has_right)
        def _():
            send(c, me + 1).wait_recv()

        whiten(c, halo.at[c], 0)
        correlate(1, c)

    back_out[1] = acc[2 * pairs : 3 * pairs, :].astype(jnp.bfloat16)

    @pl.when(has_right)
    def _():
        send_back(1, me + 1).start()
        send_back(0, me + 1).wait_recv()
        acc[pairs : 2 * pairs, :] += back_in[0].astype(jnp.float32)

    @pl.when(has_left)
    def _():
        send_back(1, me - 1).wait_recv()
        acc[pairs : 2 * pairs, :] += back_in[1].astype(jnp.float32)

    out_ref[...] = acc[pairs : 2 * pairs, :] * norm_factor
    for copy in copies:
        copy.wait_send()

    @pl.when(has_right)
    def _():
        send_pack(0, me + 1).wait_send()
        send_back(1, me + 1).wait_send()

        @pl.loop(0, half)
        def _(c):
            send(c, me + 1).wait_send()

    @pl.when(has_left)
    def _():
        send_pack(1, me - 1).wait_send()
        send_back(0, me - 1).wait_send()

        @pl.loop(half, steps)
        def _(c):
            send(c, me - 1).wait_send()


def side_own(side):
    return 1 - side


def body(spectra, pair_channels, pair_live):
    rows, windows, _, bins = spectra.shape
    count = lax.axis_size("row")
    parts = 2 * windows
    flat = spectra.reshape(rows, parts * bins)
    steps = bins // CHUNK
    tile_count, tile_pairs = pair_live.shape
    pairs = tile_count * tile_pairs
    index = jnp.transpose(pair_channels, (2, 0, 1)).reshape(2, pairs)
    packed = jnp.concatenate([index, pair_live.reshape(1, pairs)], axis=0)
    rounds = count.bit_length() - 1
    vmem = pl.BlockSpec(memory_space=pltpu.VMEM)
    dma = pltpu.SemaphoreType.DMA
    result = pl.pallas_call(
        functools.partial(kernel, count, windows, 1.0 / math.sqrt(bins * windows)),
        out_shape=jax.ShapeDtypeStruct((pairs, LAGS), jnp.float32),
        in_specs=[pl.BlockSpec(memory_space=pl.ANY), vmem],
        out_specs=vmem,
        scratch_shapes=[
            pltpu.VMEM((steps, rows, parts * CHUNK), jnp.bfloat16),
            pltpu.VMEM((steps, rows, parts * CHUNK), jnp.bfloat16),
            pltpu.VMEM((2, 3, pairs), jnp.int32),
            pltpu.VMEM((2, 2 * pairs, 2 * rows), jnp.bfloat16),
            pltpu.VMEM((2, 2 * pairs, 2 * rows), jnp.bfloat16),
            pltpu.VMEM((2 * rows, parts * CHUNK), jnp.bfloat16),
            pltpu.VMEM((2, CHUNK, LAGS), jnp.float32),
            pltpu.VMEM((3 * pairs, LAGS), jnp.float32),
            pltpu.VMEM((2, pairs, LAGS), jnp.bfloat16),
            pltpu.VMEM((2, pairs, LAGS), jnp.bfloat16),
            pltpu.VMEM((rounds + 1, steps, parts, CHUNK), jnp.float32),
            pltpu.VMEM((rounds, steps, parts, CHUNK), jnp.float32),
            dma((steps, parts)), dma((steps,)), dma((steps,)), dma((rounds,)), dma((rounds,)),
            dma((2,)), dma((2,)), dma((2,)), dma((2,)),
        ],
        compiler_params=pltpu.CompilerParams(
            collective_id=0, has_side_effects=True, vmem_limit_bytes=60 * 2**20),
    )(flat, packed)
    return result.reshape(tile_count, tile_pairs, LAGS)


def solution(mesh):
    placed = (P(("day", "row"), None, None, None), P("row", None, None), P("row", None))
    return jax.shard_map(
        body, mesh=mesh, in_specs=placed, out_specs=P(("day", "row"), None, None), check_vma=False
    )
```

```python
import functools
import math

import jax
import jax.numpy as jnp
from jax import lax
from jax.experimental import pallas as pl
from jax.experimental.pallas import tpu as pltpu
from jax.sharding import PartitionSpec as P

BAND = 64
LAGS = 512
CHUNK = 256
TILE = 512


MESH = pl.DeviceIdType.MESH


def kernel(count, windows, norm_factor, own_hbm, pack_ref, out_ref, own, halo, pack, pick_a, pick_b, white,
           base, acc, back_out, back_in, sums, heard,
           load_sem, send_sem, recv_sem, sum_send, sum_recv, pack_send, pack_recv, back_send, back_recv):
    parts = 2 * windows
    steps, rows, width = own.shape
    half = steps // 2
    chunk = width // parts
    bins = steps * chunk
    pairs = out_ref.shape[0]
    me = lax.axis_index("row")
    first_own = me * rows
    rounds = count.bit_length() - 1
    channels = count * rows
    has_left, has_right = me > 0, me < count - 1

    def load(c, k):
        return pltpu.make_async_copy(
            own_hbm.at[:, pl.ds(pl.multiple_of(k * bins + c * chunk, chunk), chunk)],
            own.at[c, :, pl.ds(k * chunk, chunk)], load_sem.at[c, k])

    def remote(src, dst, sent, got, target):
        return pltpu.make_async_remote_copy(
            src_ref=src, dst_ref=dst, send_sem=sent, recv_sem=got,
            device_id={"row": target}, device_id_type=MESH)

    def send(c, target):
        return remote(own.at[c], halo.at[c], send_sem.at[c], recv_sem.at[c], target)

    def send_pack(side, target):
        return remote(pack_ref, pack.at[side], pack_send.at[side], pack_recv.at[side], target)

    def send_back(side, target):
        return remote(back_out.at[side], back_in.at[side], back_send.at[side], back_recv.at[side], target)

    for k in range(parts):
        @pl.loop(0, steps)
        def _(c, k=k):
            load(c, k).start()

    barrier = pltpu.get_barrier_semaphore()
    partners = [me ^ (1 << r) for r in range(rounds)]
    for partner in partners:
        pl.semaphore_signal(barrier, inc=1, device_id={"row": partner}, device_id_type=MESH)
    other = lax.rem(me + 2 * lax.rem(me, 2) - 1 + count, count)
    pl.semaphore_signal(barrier, inc=1, device_id={"row": other}, device_id_type=MESH)

    acc[...] = jnp.zeros_like(acc)

    @pl.when(jnp.logical_not(has_left))
    def _():
        pack[0] = jnp.zeros(pack.shape[1:], jnp.int32)

        @pl.loop(0, half)
        def _(c):
            halo[c] = jnp.zeros((rows, width), jnp.bfloat16)

    @pl.when(jnp.logical_not(has_right))
    def _():
        pack[1] = jnp.zeros(pack.shape[1:], jnp.int32)

        @pl.loop(half, steps)
        def _(c):
            halo[c] = jnp.zeros((rows, width), jnp.bfloat16)

    @pl.loop(0, steps)
    def _(c):
        for k in range(parts):
            load(c, k).wait()
            block = own[c, :, k * chunk : (k + 1) * chunk].astype(jnp.float32)
            sums[0, c, k : k + 1, :] = jnp.sum(block, axis=0, keepdims=True)

    pl.semaphore_wait(barrier, rounds + 1)

    def add_up(r):
        copy = remote(sums.at[r], heard.at[r], sum_send.at[r], sum_recv.at[r], partners[r])
        copy.start()
        return copy

    copies = [add_up(0)]

    @pl.when(has_right)
    def _():
        send_pack(0, me + 1).start()

    @pl.when(has_left)
    def _():
        send_pack(1, me - 1).start()

    for r in range(rounds):
        if r == 0:
            shifts = lax.broadcasted_iota(jnp.int32, (chunk, LAGS), 1) + (2 * bins - LAGS // 2)
            phase = lax.rem(lax.broadcasted_iota(jnp.int32, (chunk, LAGS), 0) * shifts, 2 * bins)
            angle = phase.astype(jnp.float32) * (math.pi / bins)
            base[0] = jnp.cos(angle)
            base[1] = jnp.sin(angle)
        if r == 1:
            @pl.when(has_left)
            def _():
                send_pack(0, me - 1).wait_recv()

            @pl.when(has_right)
            def _():
                send_pack(1, me + 1).wait_recv()

            row = lax.broadcasted_iota(jnp.int32, (2 * rows, pairs), 0)
            for side in range(2):
                beside = first_own - rows if side == 0 else first_own + rows

                def pick(index, near):
                    inside = (index >= first_own) & (index < first_own + rows)
                    mine = jnp.where(inside, index - first_own + rows, -1)
                    if not near:
                        return mine
                    across = (index >= beside) & (index < beside + rows)
                    return jnp.where(across, index - beside, mine)

                for group in range(2):
                    table = pack_ref[...] if group == side_own(side) else pack[side]
                    first, second, live = table[0:1], table[1:2], table[2:3].astype(jnp.float32)
                    near = group == side_own(side)
                    at = slice(group * pairs, (group + 1) * pairs)
                    a_row = pick(first, True)
                    b_row = pick(second, near)
                    hot_a = (row == a_row).astype(jnp.float32) * live
                    hot_b = (row == b_row).astype(jnp.float32)
                    pick_a[side, at, :] = jnp.transpose(hot_a).astype(jnp.bfloat16)
                    pick_b[side, at, :] = jnp.transpose(hot_b).astype(jnp.bfloat16)
        copies[r].wait_recv()
        sums[r + 1] = sums[r] + heard[r]
        if r + 1 < rounds:
            copies.append(add_up(r + 1))

    @pl.loop(0, half)
    def _(c):
        @pl.when(has_right)
        def _():
            send(c, me + 1).start()

        @pl.when(has_left)
        def _():
            send(half + c, me - 1).start()

    lane_r = lax.broadcasted_iota(jnp.int32, (chunk, chunk), 0) // BAND
    lane_c = lax.broadcasted_iota(jnp.int32, (chunk, chunk), 1) // BAND
    same = (lane_r == lane_c).astype(jnp.float32).astype(jnp.bfloat16)

    def whiten(c, source, start):
        common = sums[rounds, c] * (1.0 / channels)
        for w in range(windows):
            at = 2 * w * chunk
            re = source[:, at : at + chunk].astype(jnp.float32) - common[2 * w : 2 * w + 1, :]
            im = source[:, at + chunk : at + 2 * chunk].astype(jnp.float32) - common[2 * w + 1 : 2 * w + 2, :]
            power = re * re + im * im
            mag = power * lax.rsqrt(jnp.maximum(power, 1e-30))
            hi = mag.astype(jnp.bfloat16)
            lo = (mag - hi.astype(jnp.float32)).astype(jnp.bfloat16)
            level = jnp.dot(hi, same, preferred_element_type=jnp.float32)
            level += jnp.dot(lo, same, preferred_element_type=jnp.float32)
            scale = 1.0 / (level * (1.0 / BAND) + 1e-06)
            white[start : start + rows, at : at + chunk] = (re * scale).astype(jnp.bfloat16)
            white[start : start + rows, at + chunk : at + 2 * chunk] = (im * scale).astype(jnp.bfloat16)

    shift_row = lax.broadcasted_iota(jnp.int32, (8, LAGS), 1) + (2 * bins - LAGS // 2)

    def correlate(side, c):
        turn = lax.rem(lax.rem(c * shift_row, 2 * bins) * chunk, 2 * bins).astype(jnp.float32) * (math.pi / bins)
        ch, sh = jnp.cos(turn)[0:1], jnp.sin(turn)[0:1]
        lag_re = (base[0] * ch - base[1] * sh).astype(jnp.bfloat16)
        lag_im = (-(base[1] * ch + base[0] * sh)).astype(jnp.bfloat16)
        tile = TILE

        @pl.loop(0, 2 * pairs // tile)
        def _(i):
            at = pl.ds(pl.multiple_of(i * tile, tile), tile)
            to = pl.ds(pl.multiple_of(side * pairs + i * tile, tile), tile)
            cross_re = jnp.zeros((tile, chunk), jnp.float32)
            cross_im = jnp.zeros((tile, chunk), jnp.float32)
            for w in range(windows):
                lo = 2 * w * chunk
                a = jnp.dot(pick_a[side, at, :], white[:, lo : lo + 2 * chunk], preferred_element_type=jnp.float32)
                b = jnp.dot(pick_b[side, at, :], white[:, lo : lo + 2 * chunk], preferred_element_type=jnp.float32)
                ar, ai, br, bi = a[:, :chunk], a[:, chunk:], b[:, :chunk], b[:, chunk:]
                cross_re += ar * br + ai * bi
                cross_im += ai * br - ar * bi
            total = jnp.dot(cross_re.astype(jnp.bfloat16), lag_re, preferred_element_type=jnp.float32)
            total += jnp.dot(cross_im.astype(jnp.bfloat16), lag_im, preferred_element_type=jnp.float32)
            acc[to, :] += total

    @pl.loop(0, half)
    def _(c):
        whiten(c, own.at[c], rows)

        @pl.when(has_left)
        def _():
            send(c, me - 1).wait_recv()

        whiten(c, halo.at[c], 0)
        correlate(0, c)
        whiten(half + c, own.at[half + c], rows)

        @pl.when(has_right)
        def _():
            send(half + c, me + 1).wait_recv()

        whiten(half + c, halo.at[half + c], 0)
        correlate(1, half + c)

    back_out[0] = acc[0:pairs, :].astype(jnp.bfloat16)

    @pl.when(has_left)
    def _():
        send_back(0, me - 1).start()

    back_out[1] = acc[2 * pairs : 3 * pairs, :].astype(jnp.bfloat16)

    @pl.when(has_right)
    def _():
        send_back(1, me + 1).start()
        send_back(0, me + 1).wait_recv()
        acc[pairs : 2 * pairs, :] += back_in[0].astype(jnp.float32)

    @pl.when(has_left)
    def _():
        send_back(1, me - 1).wait_recv()
        acc[pairs : 2 * pairs, :] += back_in[1].astype(jnp.float32)

    out_ref[...] = acc[pairs : 2 * pairs, :] * norm_factor
    for copy in copies:
        copy.wait_send()

    @pl.when(has_right)
    def _():
        send_pack(0, me + 1).wait_send()
        send_back(1, me + 1).wait_send()

        @pl.loop(0, half)
        def _(c):
            send(c, me + 1).wait_send()

    @pl.when(has_left)
    def _():
        send_pack(1, me - 1).wait_send()
        send_back(0, me - 1).wait_send()

        @pl.loop(half, steps)
        def _(c):
            send(c, me - 1).wait_send()


def side_own(side):
    return 1 - side


def body(spectra, pair_channels, pair_live):
    rows, windows, _, bins = spectra.shape
    count = lax.axis_size("row")
    parts = 2 * windows
    flat = spectra.reshape(rows, parts * bins)
    steps = bins // CHUNK
    tile_count, tile_pairs = pair_live.shape
    pairs = tile_count * tile_pairs
    index = jnp.transpose(pair_channels, (2, 0, 1)).reshape(2, pairs)
    packed = jnp.concatenate([index, pair_live.reshape(1, pairs)], axis=0)
    rounds = count.bit_length() - 1
    vmem = pl.BlockSpec(memory_space=pltpu.VMEM)
    dma = pltpu.SemaphoreType.DMA
    result = pl.pallas_call(
        functools.partial(kernel, count, windows, 1.0 / math.sqrt(bins * windows)),
        out_shape=jax.ShapeDtypeStruct((pairs, LAGS), jnp.float32),
        in_specs=[pl.BlockSpec(memory_space=pl.ANY), vmem],
        out_specs=vmem,
        scratch_shapes=[
            pltpu.VMEM((steps, rows, parts * CHUNK), jnp.bfloat16),
            pltpu.VMEM((steps, rows, parts * CHUNK), jnp.bfloat16),
            pltpu.VMEM((2, 3, pairs), jnp.int32),
            pltpu.VMEM((2, 2 * pairs, 2 * rows), jnp.bfloat16),
            pltpu.VMEM((2, 2 * pairs, 2 * rows), jnp.bfloat16),
            pltpu.VMEM((2 * rows, parts * CHUNK), jnp.bfloat16),
            pltpu.VMEM((2, CHUNK, LAGS), jnp.float32),
            pltpu.VMEM((3 * pairs, LAGS), jnp.float32),
            pltpu.VMEM((2, pairs, LAGS), jnp.bfloat16),
            pltpu.VMEM((2, pairs, LAGS), jnp.bfloat16),
            pltpu.VMEM((rounds + 1, steps, parts, CHUNK), jnp.float32),
            pltpu.VMEM((rounds, steps, parts, CHUNK), jnp.float32),
            dma((steps, parts)), dma((steps,)), dma((steps,)), dma((rounds,)), dma((rounds,)),
            dma((2,)), dma((2,)), dma((2,)), dma((2,)),
        ],
        compiler_params=pltpu.CompilerParams(
            collective_id=0, has_side_effects=True, vmem_limit_bytes=60 * 2**20),
    )(flat, packed)
    return result.reshape(tile_count, tile_pairs, LAGS)


def solution(mesh):
    placed = (P(("day", "row"), None, None, None), P("row", None, None), P("row", None))
    return jax.shard_map(
        body, mesh=mesh, in_specs=placed, out_specs=P(("day", "row"), None, None), check_vma=False
    )
```
